32 devices in a mesh: row: 4 (over y, core), col: 8 (over z, x).
Axes of the slice: x: 2, y: 2, z: 4, core: 2. Of those that a mesh axis runs over, the one named last changes fastest.
Arguments:
- a_vals: bfloat16 [256, 131072], P('row', 'col'), may hold values from -1.1953125 to 1.1953125
- p_vals: bfloat16 [64, 16384], P(None, ('row', 'col')), may hold values from -0.75 to 0.75
- a_rows: int32 [4, 2048], P('row', 'col'), may hold values from 0 to 63, as said below
- a_cols: int32 [4, 2048], P('row', 'col'), may hold values from 0 to 31, as said below
- a_count: int32 [4, 8], P('row', 'col'), may hold values from 64 to 256, as said below
- c_slot: int32 [4, 2048], P('row', 'col'), may hold values from 0 to 5, as said below
- agg: int32 [256], P(('row', 'col')), may hold values from 0 to 7, as said below
Outputs:
- coarse_vals: float32 [32, 24576], P(('row', 'col'))
The draws below stay inside these ranges and needn't reach their ends.
Inputs may be any that keep to these rules, and one draw needn't show every extreme that they name: Each tile's live slots are its first a_count ones; some tile of every row group has all 256 slots live. `agg`: in each row group, the aggregate numbers t*32//8 to (t+1)*32//8 - 1 are taken by the fine block rows of the row group's t-th column group of 32 rows, each number by exactly 8 of them. Coarse pattern: in row group r, slot k of coarse row a belongs to column group (a*6 + k + o_r) mod 8, for one shift o_r of the row group, and to one aggregate of that column group; every tile slot, live or not, has a fine row of aggregate a and a fine column of that slot's aggregate, with c_slot = k. The live slots of each tile reach every (a, k) pair of its column group. `a_rows`: see c_slot. `a_cols`: see c_slot.
All inputs are finite; a program needn't handle non-finite values.
Results may differ from the reference program's by a relative error of at most 0.0049.
Values may be sent and summed in bfloat16 or wider, within the bound.
A program may use at most 64 MiB of HBM per device.

```python
import jax
import jax.numpy as jnp
from jax import lax

BLOCK = 64
AGG = 8
KC = 6
NB = 256
RB = 64
CB = 32
KT = 256
CR = 8
NC = 32
N_ROW = 4
N_COL = 8


def draw_a_count(key, part):
    count_key, full_key = jax.random.split(key)
    counts = jax.random.randint(count_key, (N_ROW, N_COL), KT // 4, KT + 1)
    full_column = jax.random.randint(full_key, (N_ROW, 1), 0, N_COL)
    column_ids = jnp.arange(N_COL)[None, :]
    return jnp.where(column_ids == full_column, KT, counts).astype(jnp.int32)


def build_pattern(key):
    ratio = N_COL // N_ROW
    col_aggs = CB // AGG
    pairs = CR * KC // N_COL
    groups = jnp.arange(N_COL, dtype=jnp.int32)
    perm_key = jax.random.fold_in(key, 101)

    def one_perm(group):
        return jax.random.permutation(jax.random.fold_in(perm_key, group), CB).astype(jnp.int32)
    perms = jax.vmap(one_perm)(groups)
    inverse = jnp.argsort(perms, axis=1).astype(jnp.int32)
    agg_table = (groups[:, None] % ratio * col_aggs + inverse // AGG).reshape(NB).astype(jnp.int32)
    shifts = jax.random.randint(jax.random.fold_in(key, 102), (N_ROW,), 0, N_COL)
    col_choice = jax.random.randint(jax.random.fold_in(key, 103), (N_ROW, CR, KC), 0, col_aggs)
    shape = (N_ROW, N_COL, KT)
    slot_ids = jnp.arange(KT, dtype=jnp.int32)[None, None, :]
    chosen = jax.random.randint(jax.random.fold_in(key, 104), shape, 0, pairs)
    chosen = jnp.where(slot_ids < pairs, slot_ids, chosen)
    row_ids = jnp.broadcast_to(jnp.arange(N_ROW, dtype=jnp.int32)[:, None, None], shape)
    col_ids = jnp.broadcast_to(groups[None, :, None], shape)
    value = (col_ids - shifts[:, None, None]) % N_COL + chosen * N_COL
    coarse_row = value // KC
    slot_k = value % KC
    row_member = jax.random.randint(jax.random.fold_in(key, 105), shape, 0, AGG)
    owner_group = row_ids * ratio + coarse_row // col_aggs
    within = coarse_row % col_aggs * AGG + row_member
    rows = coarse_row // col_aggs * CB + perms[owner_group, within]
    target_agg = col_choice[row_ids, coarse_row, slot_k]
    col_member = jax.random.randint(jax.random.fold_in(key, 106), shape, 0, AGG)
    cols = perms[col_ids, target_agg * AGG + col_member]
    flat = (N_ROW, N_COL * KT)
    return (agg_table, rows.reshape(flat).astype(jnp.int32), cols.reshape(flat).astype(jnp.int32), slot_k.reshape(flat).astype(jnp.int32))


def draw_agg(key, part):
    return build_pattern(key)[0]


def draw_a_rows(key, part):
    return build_pattern(key)[1]


def draw_a_cols(key, part):
    return build_pattern(key)[2]


def draw_c_slot(key, part):
    return build_pattern(key)[3]


def block_levels(key, extent, pieces, least, largest):
    level, own = 1.0, jax.random.fold_in(key, 6)
    for dim, parts in pieces:
        draws = jnp.exp(jax.random.uniform(jax.random.fold_in(own, dim), (parts,), jnp.float32, least / len(pieces), largest / len(pieces)))
        level = level * jnp.repeat(draws, extent[dim] // parts).reshape([-1 if axis == dim else 1 for axis in range(len(extent))])
    return level


def bell_draw(own_key, extent, spread, limit, cuts=(), held_as=jnp.bfloat16):
    result = jax.random.normal(own_key, extent, jnp.float32) * spread
    if len(cuts) > 0:
        result = block_levels(own_key, extent, cuts, -0.22, 0.18) * result
    return jnp.clip(result, min=-limit, max=limit).astype(held_as)


def setup_inputs(seed: int = 0) -> dict:
    splits = jax.random.split(jax.random.key(seed), 8)
    a_vals = bell_draw(splits[0], (N_ROW * BLOCK, N_COL * KT * BLOCK), 0.2, 1.1953125, ((0, 4), (1, 8)))
    p_vals = bell_draw(splits[1], (BLOCK, NB * BLOCK), BLOCK ** -0.5, 0.75, ((1, 32),))
    a_rows = draw_a_rows(jax.random.fold_in(splits[7], 71), 0)
    a_cols = draw_a_cols(jax.random.fold_in(splits[7], 71), 0)
    a_count = draw_a_count(jax.random.fold_in(splits[7], 71), 0)
    c_slot = draw_c_slot(jax.random.fold_in(splits[7], 71), 0)
    agg = draw_agg(jax.random.fold_in(splits[7], 71), 0)
    return dict(a_vals=a_vals, p_vals=p_vals, a_rows=a_rows, a_cols=a_cols, a_count=a_count, c_slot=c_slot, agg=agg)


def reference(a_vals, p_vals, a_rows, a_cols, a_count, c_slot, agg):
    prolong = p_vals.reshape(BLOCK, NB, BLOCK)
    blocks_all = a_vals.reshape(N_ROW, BLOCK, N_COL, KT, BLOCK)
    segments = CR * KC

    def row_group(group_index):
        row_panel = lax.dynamic_slice_in_dim(prolong, group_index * RB, RB, 1)
        group_agg = lax.dynamic_slice_in_dim(agg, group_index * RB, RB, 0)
        group_blocks = lax.dynamic_index_in_dim(blocks_all, group_index, 0, False)
        group_rows = lax.dynamic_index_in_dim(a_rows, group_index, 0, False).reshape(N_COL, KT)
        group_cols = lax.dynamic_index_in_dim(a_cols, group_index, 0, False).reshape(N_COL, KT)
        group_slots = lax.dynamic_index_in_dim(c_slot, group_index, 0, False).reshape(N_COL, KT)
        group_counts = lax.dynamic_index_in_dim(a_count, group_index, 0, False)

        def tile(running, tile_index):
            tile_blocks = lax.dynamic_index_in_dim(group_blocks, tile_index, 1, False)
            col_panel = lax.dynamic_slice_in_dim(prolong, tile_index * CB, CB, 1)
            slot_rows = lax.dynamic_index_in_dim(group_rows, tile_index, 0, False)
            slot_cols = lax.dynamic_index_in_dim(group_cols, tile_index, 0, False)
            coarse_slot = lax.dynamic_index_in_dim(group_slots, tile_index, 0, False)
            live_count = lax.dynamic_index_in_dim(group_counts, tile_index, 0, False)
            left = jnp.take(row_panel, slot_rows, axis=1).astype(jnp.float32)
            half = jnp.einsum('fsa,fsj->saj', left, tile_blocks.astype(jnp.float32)).astype(jnp.bfloat16)
            right = jnp.take(col_panel, slot_cols, axis=1).astype(jnp.float32)
            triple = jnp.einsum('saj,jsb->sab', half.astype(jnp.float32), right).astype(jnp.bfloat16)
            live_mask = jnp.arange(KT, dtype=jnp.int32) < live_count
            target = jnp.where(live_mask, jnp.take(group_agg, slot_rows) * KC + coarse_slot, segments).astype(jnp.int32)
            summed = jax.ops.segment_sum(triple.reshape(KT, BLOCK * BLOCK).astype(jnp.float32), target, num_segments=segments + 1)[:segments]
            rounded = lax.optimization_barrier(summed.reshape(CR, KC * BLOCK * BLOCK).astype(jnp.bfloat16))
            return running + rounded.astype(jnp.float32), None

        start_value = jnp.zeros((CR, KC * BLOCK * BLOCK), jnp.float32)
        total, _ = lax.scan(tile, start_value, jnp.arange(N_COL, dtype=jnp.int32))
        return total

    return lax.map(row_group, jnp.arange(N_ROW, dtype=jnp.int32)).reshape(NC, KC * BLOCK * BLOCK)
```

```python
import functools

import jax
import jax.numpy as jnp
from jax import lax
from jax.experimental import pallas as pl
from jax.experimental.pallas import tpu as pltpu
from jax.sharding import PartitionSpec as P

AGG = 8
KC = 6
LO = 2
MESH = pl.DeviceIdType.MESH
F32 = jnp.float32
BF16 = jnp.bfloat16
I32 = jnp.int32


def iota(shape, dim):
    return lax.broadcasted_iota(I32, shape, dim)


def within(at, size):
    return jnp.minimum(jnp.maximum(at, 0), size - 1)


def bits(n):
    return n.bit_length() - 1


def sort_slots(rows_group, cols_group, small, count_v, plan_v, down_v, tag_v):
    slots = small.shape[2]
    cb, sb = bits(cols_group), bits(slots)
    rows, cols = small[0], small[1]
    lane = iota((1, slots), 1)
    key = jnp.where(lane < count_v[...], rows, rows_group)
    across = jnp.broadcast_to(((((key << cb) | cols) << sb) | lane), (slots, slots))
    side, place = iota((slots, slots), 0), iota((slots, slots), 1)
    down = jnp.sum(jnp.where(side == place, across, 0), axis=1, keepdims=True)
    rank = jnp.sum(jnp.where(across < down, 1, 0), axis=1, keepdims=True)
    more = jnp.where((across >> sb == down >> sb) & (across > down), 1, 0)
    more = jnp.sum(more, axis=1, keepdims=True)
    word = jnp.sum(jnp.where(rank == place, down, 0), axis=0, keepdims=True)
    slot, top = word & (slots - 1), word >> sb
    same = (top == pltpu.roll(top, 1, 1)) & (lane > 0)
    plan_v[0:1, :slots] = slot | (same.astype(I32) << 15)
    last = (more == 0) & (down >> (cb + sb) < rows_group)
    down_v[...] = jnp.broadcast_to(down >> sb, down_v.shape)
    tag_v[...] = jnp.broadcast_to(jnp.where(last, rank + 1, 0), tag_v.shape)


def ranks(marks, width):
    n = marks.shape[0]
    side, place = iota((n, width), 0), iota((n, width), 1)
    down = jnp.broadcast_to(marks[:, 0:1], (n, width))
    across = jnp.sum(jnp.where(side == place, down, 0), axis=0, keepdims=True)
    across = jnp.where(place[0:1] < n, across, -1)
    alike = down == across
    along = jnp.sum(jnp.where(alike & (side < place), 1, 0), axis=0, keepdims=True)
    below = jnp.sum(jnp.where(alike & (place < side), 1, 0), axis=1, keepdims=True)
    return across, along, below


def make_tables(rows_group, cols_group, slots, row_marks, col_marks, down_v, tag_v, plan_v):
    cb = bits(cols_group)
    width, wide = max(rows_group, 128), max(cols_group, 128)
    agg, place, below = ranks(row_marks, width)
    target, spot, under = ranks(col_marks, wide)
    pair = agg * AGG + place
    down = down_v[:, 0:1]
    tag = tag_v[:, 0:1]
    row, col = down >> cb, down & (cols_group - 1)
    at_row = row == iota((slots, width), 1)
    at_col = col == iota((slots, wide), 1)
    left = jnp.sum(jnp.where(at_row, pair, 0), axis=1, keepdims=True)
    right = jnp.sum(jnp.where(at_col, target * AGG + spot, 0), axis=1, keepdims=True)
    cell = left * AGG + (right & (AGG - 1))
    cells = rows_group * AGG
    step = min(cells, 512)
    for g in range(cells // step):
        q = iota((slots, step), 1) + g * step
        found = jnp.sum(jnp.where(cell == q, tag, 0), axis=0, keepdims=True)
        plan_v[1:2, g * step:(g + 1) * step] = jnp.where(found > 0, found - 1, slots)
    q = iota((rows_group, width), 1)
    mine = row_marks[:, 0:1] * AGG + below
    listed = jnp.sum(jnp.where(mine == q, iota((rows_group, width), 0), 0), axis=0, keepdims=True)
    plan_v[2:3, :width] = listed
    q = iota((slots, width), 1)
    live = (row < rows_group) & (left >> bits(AGG) == q >> bits(AGG))
    aim = jnp.max(jnp.where(live, right >> bits(AGG), -1), axis=0, keepdims=True)
    q = iota((cols_group, width), 1)
    hit = (col_marks[:, 0:1] == aim) & (under == (q & (AGG - 1)))
    listed = jnp.sum(jnp.where(hit, iota((cols_group, width), 0), 0), axis=0, keepdims=True)
    plan_v[3:4, :width] = listed


def kernel(
    n_row, n_col, a_hbm, p_hbm, rows_hbm, cols_hbm, count_hbm, kslot_hbm, agg_hbm, out_ref,
    small, count_v, agg_v, plan_v, plan_s, down_v, tag_v, agp, cgp, a_v, side, summed,
    pan, colp, flip, colb, terms, snd, rcv,
    in_sem, a_sem, plan_sem, p_send, p_recv, g_send, g_recv, c_send, c_recv, m_send, m_recv, x_send, x_recv,
):
    bw = p_hbm.shape[0]
    dev_rows = agg_v.shape[1]
    rows_group = n_col * dev_rows
    slots = small.shape[2]
    ratio = n_col // n_row
    per = n_col // ratio
    cols_group = per * dev_rows
    hi = n_col // LO
    half = bw // 2
    row = lax.axis_index("row")
    me = lax.axis_index("col")
    z, x = me // LO, lax.rem(me, LO)
    partner = z * LO + (1 - x)
    root = me // ratio
    part = lax.rem(me, ratio)
    is_root = row == root
    alike = lax.rem(row, 2) == lax.rem(root, 2)
    is_head = alike & jnp.logical_not(is_root)
    twin_row = row + 1 - 2 * lax.rem(row, 2)

    def col_of(d):
        return lax.rem(me + d, n_col)

    def row_of(d):
        return lax.rem(row + d, n_row)

    def z_of(d):
        return jnp.bitwise_xor(z, d)

    barrier = pltpu.get_barrier_semaphore()
    for d in range(1, n_col):
        pl.semaphore_signal(barrier, inc=1, device_id=(row, col_of(d)), device_id_type=MESH)
    for d in range(1, n_row):
        pl.semaphore_signal(barrier, inc=1, device_id=(row_of(d), me), device_id_type=MESH)
    loads = [
        pltpu.make_async_copy(src, dst, in_sem.at[i])
        for i, (src, dst) in enumerate(
            [
                (agg_hbm, agg_v),
                (rows_hbm, small.at[0]),
                (cols_hbm, small.at[1]),
                (count_hbm, count_v),
                (kslot_hbm, small.at[2]),
                (p_hbm, pan.at[me]),
            ]
        )
    ]
    for c in loads:
        c.start()
    pl.semaphore_wait(barrier, n_col + n_row - 2)

    def remote(src, dst, s, r, dev):
        return pltpu.make_async_remote_copy(
            src_ref=src, dst_ref=dst, send_sem=s, recv_sem=r, device_id=dev, device_id_type=MESH
        )

    own = [remote(p_hbm, pan.at[me], p_send.at[0], p_recv.at[me], (row, partner))]
    for d in range(1, hi):
        own.append(
            remote(p_hbm, pan.at[me], p_send.at[d], p_recv.at[me], (row, z_of(d) * LO + x))
        )
    for c in own:
        c.start()

    def panel_copies(q, src):
        m = lax.rem(q, per)
        copies = [remote(src, colp.at[m], c_send.at[m, 0], c_recv.at[m], (twin_row, me))]
        for d in range(1, n_row // 2):
            copies.append(
                remote(src, colp.at[m], c_send.at[m, d], c_recv.at[m], (row_of(2 * d), me))
            )
        return copies

    def hand_on(q, src):
        @pl.when(is_root & (q // per == part))
        def _():
            for c in reversed(panel_copies(q, src)):
                c.start()

    hand_on(me, p_hbm)

    @pl.loop(0, slots // 16)
    def _(g):
        for u in range(8):
            i = g * 8 + u
            lanes = pl.ds(pl.multiple_of(i * (2 * bw), 2 * bw), 2 * bw)
            pltpu.make_async_copy(a_hbm.at[:, lanes], a_v.at[i], a_sem).start()

    loads[0].wait()
    square = (dev_rows, dev_rows)
    eye = iota(square, 0) == iota(square, 1)
    mine = jnp.where(eye, jnp.broadcast_to(agg_v[...], square), 0)
    mine = jnp.sum(mine, axis=1, keepdims=True)
    agp[me] = jnp.broadcast_to(mine, agp.shape[1:])
    marks = [
        remote(agp.at[me], agp.at[me], g_send.at[d - 1], g_recv.at[me], (row, col_of(d)))
        for d in range(1, n_col)
    ]
    for c in marks:
        c.start()
    for c in loads[1:]:
        c.wait()
    sort_slots(rows_group, cols_group, small, count_v, plan_v, down_v, tag_v)
    plan_copy = pltpu.make_async_copy(plan_v, plan_s, plan_sem)
    plan_copy.start()
    lanes = iota((bw, 2 * bw), 1)
    side[0] = (lanes < bw).astype(F32).astype(BF16)
    side[1] = (lanes >= bw).astype(F32).astype(BF16)
    summed[slots] = jnp.zeros((bw, 2 * bw), BF16)

    def landed(q):
        remote(p_hbm, pan.at[q], p_send.at[0], p_recv.at[q], (row, partner)).wait_recv()

    def turn(q):
        for h in range(dev_rows // 2):
            t = pan[q, :, 2 * h * bw:2 * (h + 1) * bw].T
            for e in range(2):
                block = t[e * bw:(e + 1) * bw]
                flip[q * dev_rows + 2 * h + e] = jnp.concatenate([block, block], axis=1)

    pltpu.make_async_copy(a_v, a_v, a_sem).wait()

    plan_copy.wait()

    def sums(lo, hi_, acc):
        def body(i, acc):
            for u in range(8):
                word = plan_s[0, 8 * i + u]
                keep = ((word >> 15) & 1).astype(F32)
                pair = a_v[(word & (slots - 1)) >> 1] * side[word & 1]
                acc = acc * keep + pair.astype(F32)
                summed[8 * i + u] = acc.astype(BF16)
            return acc

        return lax.fori_loop(lo, hi_, body, acc)

    landed(partner)
    hand_on(partner, pan.at[partner])
    turn(me)
    turn(partner)
    acc = sums(0, slots // 16, jnp.zeros((bw, 2 * bw), F32))
    passed = []
    for d in range(1, hi):
        q = z_of(d) * LO + x
        landed(q)
        c = remote(pan.at[q], pan.at[q], p_send.at[hi - 1 + d], p_recv.at[q], (row, partner))
        c.start()
        passed.append(c)
        hand_on(q, pan.at[q])
        turn(q)
    acc = sums(slots // 16, slots // 8, acc)

    for d in range(1, n_col):
        q = col_of(d)
        remote(agp.at[q], agp.at[q], g_send.at[0], g_recv.at[q], (row, partner)).wait_recv()

    @pl.when(is_root)
    def _():
        for m in range(per):
            cgp[m] = agp[part * per + m]

    def mark_copies():
        return [
            remote(cgp, cgp, m_send.at[d - 1], m_recv, (row_of(d), me)) for d in range(1, n_row)
        ]

    @pl.when(is_root)
    def _():
        for c in mark_copies():
            c.start()

    for d in range(1, hi):
        q = z_of(d) * LO + (1 - x)
        landed(q)
        hand_on(q, pan.at[q])
        turn(q)

    @pl.when(jnp.logical_not(is_root))
    def _():
        remote(cgp, cgp, m_send.at[0], m_recv, (row, partner)).wait_recv()

    row_marks = jnp.concatenate([agp[c] for c in range(n_col)], axis=0)
    col_marks = jnp.concatenate([cgp[m] for m in range(per)], axis=0)
    make_tables(rows_group, cols_group, slots, row_marks, col_marks, down_v, tag_v, plan_v)
    there = iota((rows_group, 2 * bw), 0) == small[0, 0:1, 0:1]
    first = jnp.sum(jnp.where(there, row_marks, 0), axis=0, keepdims=True)
    first = first * KC + small[2, 0:1, 0:1]
    plan_copy.start()
    plan_copy.wait()

    in_left = (iota((bw, 2 * bw), 1) < bw).astype(F32).astype(BF16)
    in_right = (iota((bw, 2 * bw), 1) >= bw).astype(F32).astype(BF16)

    def join(left, right):
        return left * in_left + right * in_right

    def unpack(m, src):
        for b in range(dev_rows):
            colb[m * dev_rows + b] = src[:, b * bw:(b + 1) * bw]

    for m in range(per):
        @pl.when(is_root)
        def _():
            unpack(m, pan.at[part * per + m])

        @pl.when(jnp.logical_not(is_root))
        def _():
            remote(
                p_hbm, colp.at[m], c_send.at[m, 0], c_recv.at[m], (row, partner)
            ).wait_recv()

            @pl.when(is_head)
            def _():
                panel_copies(m, colp.at[m])[0].start()

            unpack(m, colp.at[m])

    aggs = rows_group // AGG
    block = min(aggs, 8)

    def fold(g, carry):
        for u in range(block):
            a = g * block + u
            right = jnp.concatenate(
                [colb[plan_s[3, a * AGG + n // 2]] for n in range(2 * AGG)], axis=0
            )
            mat = jnp.concatenate(
                [
                    jnp.concatenate(
                        [summed[plan_s[1, (a * AGG + m) * AGG + n]] for n in range(AGG)], axis=1
                    )
                    for m in range(AGG)
                ],
                axis=0,
            )
            left = jnp.concatenate(
                [
                    join(
                        flip[plan_s[2, a * AGG + 2 * h]],
                        flip[plan_s[2, a * AGG + 2 * h + 1]],
                    )
                    for h in range(AGG // 2)
                ],
                axis=1,
            )
            mid = jnp.dot(left, mat, preferred_element_type=F32).astype(BF16)
            terms[a] = jnp.dot(mid, right, preferred_element_type=F32)
        for u in range(block):
            a = g * block + u
            even = terms[a, pl.ds(0, half, stride=2), :]
            odd = terms[a, pl.ds(1, half, stride=2), :]
            snd[a] = jnp.concatenate([even, odd], axis=1).astype(BF16)
        return carry

    lax.fori_loop(0, aggs // block, fold, 0)

    def term(o):
        return remote(snd.at[o], rcv.at[me], x_send.at[o], x_recv.at[me], (row, o))

    for o in range(n_col):
        @pl.when(me != o)
        def _():
            term(o).start()

    rcv[me] = snd[me]
    for d in range(1, n_col):
        q = col_of(d)
        remote(snd.at[0], rcv.at[q], x_send.at[0], x_recv.at[q], (row, partner)).wait_recv()
    total = [jnp.zeros((half, 2 * bw), F32) for _ in range(KC)]
    for c in range(n_col):
        value = rcv[c].astype(F32)
        where = (first + (c - (KC + 1) * me + 8 * n_col * n_col)) & (n_col - 1)
        for k in range(KC):
            total[k] += jnp.where(where == k, value, 0.0)
    for k in range(KC):
        out_ref[k * half:(k + 1) * half, :] = total[k].astype(BF16)

    for c in own + passed + marks:
        c.wait_send()
    for o in range(n_col):
        @pl.when(me != o)
        def _():
            term(o).wait_send()

    @pl.when(is_root)
    def _():
        for c in mark_copies():
            c.wait_send()
        for m in range(per):
            for c in panel_copies(m, pan.at[0]):
                c.wait_send()

    @pl.when(is_head)
    def _():
        for m in range(per):
            panel_copies(m, colp.at[m])[0].wait_send()


def on_device(n_row, n_col, a_vals, p_vals, a_rows, a_cols, a_count, c_slot, agg):
    bw = p_vals.shape[0]
    dev_rows = agg.shape[0]
    slots = a_rows.shape[1]
    rows_group = dev_rows * n_col
    ratio = n_col // n_row
    per = n_col // ratio
    cols_group = per * dev_rows
    hi = n_col // LO
    assert rows_group // AGG == n_col and n_col >= KC and n_row % 2 == 0
    assert all(n & (n - 1) == 0 for n in (n_col, slots, cols_group, dev_rows, hi))
    keep = pl.BlockSpec(memory_space=pltpu.HBM)
    vmem = pl.BlockSpec(memory_space=pltpu.VMEM)
    dma = pltpu.SemaphoreType.DMA
    cells = max(slots, rows_group * AGG)
    out = pl.pallas_call(
        functools.partial(kernel, n_row, n_col),
        out_shape=jax.ShapeDtypeStruct((KC * bw // 2, 2 * bw), BF16),
        in_specs=[keep] * 7,
        out_specs=vmem,
        scratch_shapes=[
            pltpu.VMEM((3, 1, slots), I32),
            pltpu.VMEM((1, 1), I32),
            pltpu.VMEM((1, dev_rows), I32),
            pltpu.VMEM((8, cells), I32),
            pltpu.SMEM((8, cells), I32),
            pltpu.VMEM((slots, 128), I32),
            pltpu.VMEM((slots, 128), I32),
            pltpu.VMEM((n_col, dev_rows, 128), I32),
            pltpu.VMEM((per, dev_rows, 128), I32),
            pltpu.VMEM((slots // 2, bw, 2 * bw), BF16),
            pltpu.VMEM((2, bw, 2 * bw), BF16),
            pltpu.VMEM((slots + 1, bw, 2 * bw), BF16),
            pltpu.VMEM((n_col, bw, dev_rows * bw), BF16),
            pltpu.VMEM((per, bw, dev_rows * bw), BF16),
            pltpu.VMEM((rows_group, bw, 2 * bw), BF16),
            pltpu.VMEM((cols_group, bw, bw), BF16),
            pltpu.VMEM((n_col, bw, bw), F32),
            pltpu.VMEM((n_col, bw // 2, 2 * bw), BF16),
            pltpu.VMEM((n_col, bw // 2, 2 * bw), BF16),
            dma((6,)), dma, dma,
            dma((2 * hi,)), dma((n_col,)),
            dma((n_col,)), dma((n_col,)),
            dma((per, n_row // 2)), dma((per,)),
            dma((n_row,)), dma,
            dma((n_col,)), dma((n_col,)),
        ],
        compiler_params=pltpu.CompilerParams(
            collective_id=0, has_side_effects=True, vmem_limit_bytes=67043328
        ),
    )(a_vals, p_vals, a_rows, a_cols, a_count, c_slot, agg.reshape(1, dev_rows))
    return out.astype(F32).reshape(1, KC * bw * bw)


def solution(mesh):
    return jax.shard_map(
        functools.partial(on_device, mesh.shape["row"], mesh.shape["col"]),
        mesh=mesh,
        in_specs=(
            P("row", "col"),
            P(None, ("row", "col")),
            P("row", "col"),
            P("row", "col"),
            P("row", "col"),
            P("row", "col"),
            P(("row", "col")),
        ),
        out_specs=P(("row", "col"), None),
        check_vma=False,
    )
```

```python
import functools
import math

import jax
import jax.numpy as jnp
from jax import lax
from jax.experimental import pallas as pl
from jax.experimental.pallas import tpu as pltpu
from jax.sharding import PartitionSpec as P

AGG = 8
KC = 6
LO = 2
MESH = pl.DeviceIdType.MESH
F32 = jnp.float32
BF16 = jnp.bfloat16
I32 = jnp.int32


def iota(shape, dim):
    return lax.broadcasted_iota(I32, shape, dim)


def within(at, size):
    return jnp.minimum(jnp.maximum(at, 0), size - 1)


def bits(n):
    return n.bit_length() - 1


def make_plan(rows_group, cols_group, ratio, small, count_v, plan_v):
    slots = small.shape[2]
    rb, cb, sb, ab = bits(rows_group), bits(cols_group), bits(slots), bits(AGG)
    groups = KC
    rows, cols = small[0], small[1]
    lane = iota((1, slots), 1)
    group = (rows >> cb) * (KC // ratio) + (small[2] >> bits(ratio))
    group = jnp.where(lane < count_v[...], group, groups)
    key = ((((group << rb) | rows) << cb | cols) << sb) | lane
    across = jnp.broadcast_to(key, (slots, slots))
    side, place = iota((slots, slots), 0), iota((slots, slots), 1)
    down = jnp.sum(jnp.where(side == place, across, 0), axis=1, keepdims=True)
    less = across < down
    rank = jnp.sum(jnp.where(less, 1, 0), axis=1, keepdims=True)
    cell_a, cell_d = key >> sb, down >> sb
    more = jnp.sum(jnp.where((cell_a == cell_d) & (across > down), 1, 0), axis=1, keepdims=True)
    word = jnp.sum(jnp.where(rank == place, down, 0), axis=0, keepdims=True)
    top = word >> sb
    same = (top == pltpu.roll(top, 1, 1)) & (lane > 0)
    word = (word & (slots - 1)) | (same.astype(I32) << 15)
    for g in range(slots // 128):
        plan_v[g:g + 1, :] = word[:, g * 128:(g + 1) * 128]

    def spots(line, n):
        line_a = (group << n) | line
        line_d = jnp.sum(jnp.where(side == place, line_a, 0), axis=1, keepdims=True)
        other = jnp.where((line_d == line_a) & (down < across), 1, 0)
        line_a = jnp.where(jnp.sum(other, axis=0, keepdims=True) == 0, line_a, -1)
        mine = (line_a < line_d) & (line_a >= (line_d >> n) << n)
        return line_d, jnp.sum(jnp.where(mine, 1, 0), axis=1, keepdims=True)

    line, down_at = spots(rows, rb)
    post, over_at = spots(cols, cb)
    group = line >> rb
    cell = (((group << ab) | down_at) << ab) | over_at
    tag = jnp.where((more == 0) & (group < groups), rank + 1, 0)
    at = slots // 128
    q = iota((slots, 128), 1)
    for g in range(groups * AGG * AGG // 128):
        found = jnp.sum(jnp.where(cell == q + g * 128, tag, 0), axis=0, keepdims=True)
        plan_v[at + g:at + g + 1, :] = jnp.where(found > 0, found - 1, slots)
    at += groups * AGG * AGG // 128
    line = jnp.where((group << ab) + down_at == q, line & (rows_group - 1), 0)
    post = jnp.where((group << ab) + over_at == q, post & (cols_group - 1), 0)
    line = jnp.max(line, axis=0, keepdims=True)
    post = jnp.max(post, axis=0, keepdims=True)
    plan_v[at:at + 1, :] = line | (post << 16)


def kernel(
    n_row, n_col, a_hbm, p_hbm, rows_hbm, cols_hbm, count_hbm, kslot_hbm, agg_hbm, out_ref,
    small, count_v, agg_v, plan_v, plan_s, from_v, from_s, agp, a_v, side, summed,
    pan, colp, flip, colb, mids, terms, packed, snd, rcv,
    in_sem, a_sem, plan_sem, from_sem, p_send, p_recv, g_send, g_recv, c_send, c_recv, x_send, x_recv,
):
    bw = p_hbm.shape[0]
    dev_rows = agg_v.shape[1]
    rows_group = n_col * dev_rows
    slots = small.shape[2]
    ratio = n_col // n_row
    per = n_col // ratio
    cols_group = per * dev_rows
    hi = n_col // LO
    half = bw // 2
    row = lax.axis_index("row")
    me = lax.axis_index("col")
    z, x = me // LO, lax.rem(me, LO)
    partner = z * LO + (1 - x)
    root = me // ratio
    part = lax.rem(me, ratio)
    is_root = row == root
    alike = lax.rem(row, 2) == lax.rem(root, 2)
    is_head = alike & jnp.logical_not(is_root)
    twin_row = row + 1 - 2 * lax.rem(row, 2)

    def col_of(d):
        return lax.rem(me + d, n_col)

    def row_of(d):
        return lax.rem(row + d, n_row)

    def z_of(d):
        return jnp.bitwise_xor(z, d)

    barrier = pltpu.get_barrier_semaphore()
    for d in range(1, n_col):
        pl.semaphore_signal(barrier, inc=1, device_id=(row, col_of(d)), device_id_type=MESH)
    for d in range(1, n_row):
        pl.semaphore_signal(barrier, inc=1, device_id=(row_of(d), me), device_id_type=MESH)
    loads = [
        pltpu.make_async_copy(src, dst, in_sem.at[i])
        for i, (src, dst) in enumerate(
            [
                (agg_hbm, agg_v),
                (rows_hbm, small.at[0]),
                (cols_hbm, small.at[1]),
                (count_hbm, count_v),
                (kslot_hbm, small.at[2]),
                (p_hbm, pan.at[me]),
            ]
        )
    ]
    for c in loads:
        c.start()
    pl.semaphore_wait(barrier, n_col + n_row - 2)

    def remote(src, dst, s, r, dev):
        return pltpu.make_async_remote_copy(
            src_ref=src, dst_ref=dst, send_sem=s, recv_sem=r, device_id=dev, device_id_type=MESH
        )

    def send_own(do):
        for d in range(1, hi):
            to = z_of(d) * LO + jnp.where(z_of(d) == row, me // per, x)
            do(remote(p_hbm, pan.at[me], p_send.at[d], p_recv.at[me], (row, to)))

    own = [remote(p_hbm, pan.at[me], p_send.at[3 * hi - 1], p_recv.at[me], (row, partner))]
    own[0].start()
    send_own(lambda c: c.start())

    def panel_copies(q, src):
        m = lax.rem(q, per)
        copies = [remote(src, colp.at[m], c_send.at[m, 0], c_recv.at[m], (twin_row, me))]
        for d in range(1, n_row // 2):
            copies.append(
                remote(src, colp.at[m], c_send.at[m, d], c_recv.at[m], (row_of(2 * d), me))
            )
        return copies

    def twin_copy(m):
        return remote(colp.at[m], colp.at[m], c_send.at[m, 0], c_recv.at[m], (twin_row, me))

    def panel_landed(m):
        remote(
            p_hbm, colp.at[m], c_send.at[m, 0], c_recv.at[m], (row, partner)
        ).wait_recv()

    def hand_on(q, src):
        @pl.when(is_root & (q // per == part))
        def _():
            for c in reversed(panel_copies(q, src)):
                c.start()

    hand_on(me, p_hbm)

    @pl.loop(0, slots // 16)
    def _(g):
        for u in range(8):
            i = g * 8 + u
            lanes = pl.ds(pl.multiple_of(i * (2 * bw), 2 * bw), 2 * bw)
            pltpu.make_async_copy(a_hbm.at[:, lanes], a_v.at[i], a_sem).start()

    loads[0].wait()
    square = (dev_rows, dev_rows)
    eye = iota(square, 0) == iota(square, 1)
    mine = jnp.where(eye, jnp.broadcast_to(agg_v[...], square), 0)
    mine = jnp.sum(mine, axis=1, keepdims=True)
    agp[me] = jnp.broadcast_to(mine, agp.shape[1:])
    marks = [
        remote(agp.at[me], agp.at[me], g_send.at[d - 1], g_recv.at[me], (row, col_of(d)))
        for d in range(1, n_col)
    ]
    for c in marks:
        c.start()
    for c in loads[1:]:
        c.wait()
    make_plan(rows_group, cols_group, ratio, small, count_v, plan_v)
    plan_copy = pltpu.make_async_copy(plan_v, plan_s, plan_sem)
    plan_copy.start()
    lanes = iota((bw, 2 * bw), 1)
    side[0] = (lanes < bw).astype(F32).astype(BF16)
    side[1] = (lanes >= bw).astype(F32).astype(BF16)
    summed[slots] = jnp.zeros((bw, 2 * bw), BF16)

    def landed(q):
        remote(p_hbm, pan.at[q], p_send.at[0], p_recv.at[q], (row, partner)).wait_recv()

    blank = jnp.zeros((bw, bw), BF16)

    def turn(q):
        for h in range(dev_rows // 2):
            t = pan[q, :, 2 * h * bw:2 * (h + 1) * bw].T
            for e in range(2):
                block, at = t[e * bw:(e + 1) * bw], q * dev_rows + 2 * h + e
                flip[2 * at] = jnp.concatenate([block, blank], axis=1)
                flip[2 * at + 1] = jnp.concatenate([blank, block], axis=1)

    pltpu.make_async_copy(a_v, a_v, a_sem).wait()

    plan_copy.wait()

    def sums(lo, hi_, acc):
        def body(i, acc):
            for u in range(8):
                word = plan_s[i >> 4, ((i & 15) << 3) + u]
                keep = ((word >> 15) & 1).astype(F32)
                pair = a_v[(word & (slots - 1)) >> 1] * side[word & 1]
                acc = acc * keep + pair.astype(F32)
                summed[8 * i + u] = acc.astype(BF16)
            return acc

        return lax.fori_loop(lo, hi_, body, acc)

    turn(me)
    acc = sums(0, slots // 16, jnp.zeros((bw, 2 * bw), F32))
    landed(partner)
    hand_on(partner, pan.at[partner])
    def pair(d):
        q = z_of(d) * LO + x
        return q, q + 1 - 2 * x, is_root & (q // per == x)

    def relay(q, at):
        return remote(pan.at[q], pan.at[q], p_send.at[at], p_recv.at[q], (row, partner))

    for d in range(1, hi):
        q, other, both = pair(d)

        @pl.when(both | jnp.logical_not(is_root))
        def _():
            landed(q)
            relay(q, hi - 1 + d).start()
            hand_on(q, pan.at[q])

        @pl.when(both)
        def _():
            landed(other)
            relay(other, 2 * hi - 1 + d).start()
            hand_on(other, pan.at[other])

    turn(partner)
    for d in range(1, hi):
        q, other, both = pair(d)

        @pl.when(both | jnp.logical_not(is_root))
        def _():
            turn(q)

        @pl.when(both)
        def _():
            turn(other)

    acc = sums(slots // 16, slots // 8, acc)
    for d in range(1, hi):
        q, other, both = pair(d)

        @pl.when(is_root & jnp.logical_not(both))
        def _():
            landed(q)
            turn(q)

        @pl.when(jnp.logical_not(both))
        def _():
            landed(other)
            turn(other)

    @pl.when(is_head)
    def _():
        for m in range(per):
            panel_landed(m)
            twin_copy(m).start()

    cells, lists = slots // 128, slots // 128 + KC * AGG * AGG // 128

    def listed(p, m):
        return plan_s[lists, p * AGG + m]

    for p in range(KC):
        left = jnp.concatenate(
            [
                flip[2 * (listed(p, 2 * h) & (rows_group - 1))]
                + flip[2 * (listed(p, 2 * h + 1) & (rows_group - 1)) + 1]
                for h in range(AGG // 2)
            ],
            axis=1,
        )

        def cell(m, n):
            at = (p * AGG + m) * AGG + n
            return summed[plan_s[cells + at // 128, at % 128]]

        mat = jnp.concatenate(
            [jnp.concatenate([cell(m, n) for n in range(AGG)], axis=1) for m in range(AGG)], axis=0
        )
        mids[p] = jnp.dot(left, mat, preferred_element_type=F32).astype(BF16)

    for d in range(1, n_col):
        q = col_of(d)
        remote(agp.at[q], agp.at[q], g_send.at[0], g_recv.at[q], (row, partner)).wait_recv()

    row_marks = jnp.concatenate([agp[c] for c in range(n_col)], axis=0)
    there = iota((rows_group, 2 * bw), 0) == small[0, 0:1, 0:1]
    first = jnp.sum(jnp.where(there, row_marks, 0), axis=0, keepdims=True)
    first = first * KC + small[2, 0:1, 0:1]
    owner = iota((1, 2 * bw), 1)
    slot = (first - KC * owner + 8 * n_col * n_col) & (n_col - 1)
    holds = (owner >> bits(per)) * (KC // ratio) + (slot >> bits(ratio))
    from_v[...] = jnp.where(slot < KC, holds, 0)
    from_copy = pltpu.make_async_copy(from_v, from_s, from_sem)
    from_copy.start()
    def unpack(m, src):
        for b in range(dev_rows):
            colb[m * dev_rows + b] = src[:, b * bw:(b + 1) * bw]

    for m in range(per):
        @pl.when(is_root)
        def _():
            unpack(m, pan.at[part * per + m])

        @pl.when(jnp.logical_not(is_root))
        def _():
            @pl.when(jnp.logical_not(is_head))
            def _():
                panel_landed(m)

            unpack(m, colp.at[m])

    for p in range(KC):
        right = jnp.concatenate(
            [colb[(listed(p, n // 2) >> 16) & (cols_group - 1)] for n in range(2 * AGG)], axis=0
        )
        terms[p] = jnp.dot(mids[p], right, preferred_element_type=F32)
    for p in range(KC):
        even = terms[p, pl.ds(0, half, stride=2), :]
        odd = terms[p, pl.ds(1, half, stride=2), :]
        packed[p] = jnp.concatenate([even, odd], axis=1).astype(BF16)
    from_copy.wait()
    for o in range(n_col):
        snd[o] = packed[within(from_s[0, o], KC)]

    def term(o):
        return remote(snd.at[o], rcv.at[me], x_send.at[o], x_recv.at[me], (row, o))

    for o in range(n_col):
        @pl.when(me != o)
        def _():
            term(o).start()

    rcv[me] = snd[me]
    for d in range(1, n_col):
        q = col_of(d)
        remote(snd.at[0], rcv.at[q], x_send.at[0], x_recv.at[q], (row, partner)).wait_recv()
    total = [jnp.zeros((half, 2 * bw), F32) for _ in range(KC)]
    for c in range(n_col):
        value = rcv[c].astype(F32)
        where = (first + (c - (KC + 1) * me + 8 * n_col * n_col)) & (n_col - 1)
        for k in range(KC):
            total[k] += jnp.where(where == k, value, 0.0)
    for k in range(KC):
        out_ref[k * half:(k + 1) * half, :] = total[k].astype(BF16)

    for c in own + marks:
        c.wait_send()
    for d in range(1, hi):
        q, other, both = pair(d)

        @pl.when(both | jnp.logical_not(is_root))
        def _():
            relay(q, hi - 1 + d).wait_send()

        @pl.when(both)
        def _():
            relay(other, 2 * hi - 1 + d).wait_send()

    send_own(lambda c: c.wait_send())
    for o in range(n_col):
        @pl.when(me != o)
        def _():
            term(o).wait_send()

    @pl.when(is_root)
    def _():
        for m in range(per):
            for c in panel_copies(m, pan.at[0]):
                c.wait_send()

    @pl.when(is_head)
    def _():
        for m in range(per):
            twin_copy(m).wait_send()


def on_device(n_row, n_col, a_vals, p_vals, a_rows, a_cols, a_count, c_slot, agg):
    bw = p_vals.shape[0]
    dev_rows = agg.shape[0]
    slots = a_rows.shape[1]
    rows_group = dev_rows * n_col
    ratio = n_col // n_row
    per = n_col // ratio
    cols_group = per * dev_rows
    hi = n_col // LO
    assert rows_group // AGG == n_col and n_col >= KC and n_row % 2 == 0
    assert ratio == LO and hi == n_row
    assert math.gcd(KC, n_col) == ratio and slots % 128 == 0 and 2 * bw == 128
    assert all(n & (n - 1) == 0 for n in (n_col, slots, cols_group, dev_rows, hi))
    keep = pl.BlockSpec(memory_space=pltpu.HBM)
    vmem = pl.BlockSpec(memory_space=pltpu.VMEM)
    dma = pltpu.SemaphoreType.DMA
    out = pl.pallas_call(
        functools.partial(kernel, n_row, n_col),
        out_shape=jax.ShapeDtypeStruct((KC * bw // 2, 2 * bw), BF16),
        in_specs=[keep] * 7,
        out_specs=vmem,
        scratch_shapes=[
            pltpu.VMEM((3, 1, slots), I32),
            pltpu.VMEM((1, 1), I32),
            pltpu.VMEM((1, dev_rows), I32),
            pltpu.VMEM((8, 128), I32),
            pltpu.SMEM((8, 128), I32),
            pltpu.VMEM((1, 128), I32),
            pltpu.SMEM((1, 128), I32),
            pltpu.VMEM((n_col, dev_rows, 128), I32),
            pltpu.VMEM((slots // 2, bw, 2 * bw), BF16),
            pltpu.VMEM((2, bw, 2 * bw), BF16),
            pltpu.VMEM((slots + 1, bw, 2 * bw), BF16),
            pltpu.VMEM((n_col, bw, dev_rows * bw), BF16),
            pltpu.VMEM((per, bw, dev_rows * bw), BF16),
            pltpu.VMEM((2 * rows_group, bw, 2 * bw), BF16),
            pltpu.VMEM((cols_group, bw, bw), BF16),
            pltpu.VMEM((KC, bw, 2 * AGG * bw), BF16),
            pltpu.VMEM((KC, bw, bw), F32),
            pltpu.VMEM((KC, bw // 2, 2 * bw), BF16),
            pltpu.VMEM((n_col, bw // 2, 2 * bw), BF16),
            pltpu.VMEM((n_col, bw // 2, 2 * bw), BF16),
            dma((6,)), dma, dma, dma,
            dma((3 * hi,)), dma((n_col,)),
            dma((n_col,)), dma((n_col,)),
            dma((per, n_row // 2)), dma((per,)),
            dma((n_col,)), dma((n_col,)),
        ],
        compiler_params=pltpu.CompilerParams(
            collective_id=0, has_side_effects=True, vmem_limit_bytes=67043328
        ),
    )(a_vals, p_vals, a_rows, a_cols, a_count, c_slot, agg.reshape(1, dev_rows))
    return out.astype(F32).reshape(1, KC * bw * bw)


def solution(mesh):
    return jax.shard_map(
        functools.partial(on_device, mesh.shape["row"], mesh.shape["col"]),
        mesh=mesh,
        in_specs=(
            P("row", "col"),
            P(None, ("row", "col")),
            P("row", "col"),
            P("row", "col"),
            P("row", "col"),
            P("row", "col"),
            P(("row", "col")),
        ),
        out_specs=P(("row", "col"), None),
        check_vma=False,
    )
```

```python
import functools
import math

import jax
import jax.numpy as jnp
from jax import lax
from jax.experimental import pallas as pl
from jax.experimental.pallas import tpu as pltpu
from jax.sharding import PartitionSpec as P

AGG = 8
KC = 6
LO = 2
MESH = pl.DeviceIdType.MESH
F32 = jnp.float32
BF16 = jnp.bfloat16
I32 = jnp.int32


def iota(shape, dim):
    return lax.broadcasted_iota(I32, shape, dim)


def within(at, size):
    return jnp.minimum(jnp.maximum(at, 0), size - 1)


def bits(n):
    return n.bit_length() - 1


def make_plan(rows_group, cols_group, ratio, small, count_v, plan_v):
    slots = small.shape[2]
    rb, cb, sb, ab = bits(rows_group), bits(cols_group), bits(slots), bits(AGG)
    groups = KC
    rows, cols = small[0], small[1]
    lane = iota((1, slots), 1)
    group = (rows >> cb) * (KC // ratio) + (small[2] >> bits(ratio))
    group = jnp.where(lane < count_v[...], group, groups)
    key = ((((group << rb) | rows) << cb | cols) << sb) | lane
    across = jnp.broadcast_to(key, (slots, slots))
    side, place = iota((slots, slots), 0), iota((slots, slots), 1)
    down = jnp.sum(jnp.where(side == place, across, 0), axis=1, keepdims=True)
    less = across < down
    rank = jnp.sum(jnp.where(less, 1, 0), axis=1, keepdims=True)
    cell_a, cell_d = key >> sb, down >> sb
    more = jnp.sum(jnp.where((cell_a == cell_d) & (across > down), 1, 0), axis=1, keepdims=True)
    word = jnp.sum(jnp.where(rank == place, down, 0), axis=0, keepdims=True)
    top = word >> sb
    same = (top == pltpu.roll(top, 1, 1)) & (lane > 0)
    word = (word & (slots - 1)) | (same.astype(I32) << 15)
    for g in range(slots // 128):
        plan_v[g:g + 1, :] = word[:, g * 128:(g + 1) * 128]

    def spots(line, n):
        line_a = (group << n) | line
        line_d = jnp.sum(jnp.where(side == place, line_a, 0), axis=1, keepdims=True)
        other = jnp.where((line_d == line_a) & (down < across), 1, 0)
        line_a = jnp.where(jnp.sum(other, axis=0, keepdims=True) == 0, line_a, -1)
        mine = (line_a < line_d) & (line_a >= (line_d >> n) << n)
        return line_d, jnp.sum(jnp.where(mine, 1, 0), axis=1, keepdims=True)

    line, down_at = spots(rows, rb)
    post, over_at = spots(cols, cb)
    group = line >> rb
    cell = (((group << ab) | down_at) << ab) | over_at
    tag = jnp.where((more == 0) & (group < groups), rank + 1, 0)
    at = slots // 128
    q = iota((slots, 128), 1)
    for g in range(groups * AGG * AGG // 128):
        found = jnp.sum(jnp.where(cell == q + g * 128, tag, 0), axis=0, keepdims=True)
        plan_v[at + g:at + g + 1, :] = jnp.where(found > 0, found - 1, slots)
    at += groups * AGG * AGG // 128
    line = jnp.where((group << ab) + down_at == q, line & (rows_group - 1), 0)
    post = jnp.where((group << ab) + over_at == q, post & (cols_group - 1), 0)
    line = jnp.max(line, axis=0, keepdims=True)
    post = jnp.max(post, axis=0, keepdims=True)
    plan_v[at:at + 1, :] = line | (post << 16)


def kernel(
    n_row, n_col, a_hbm, p_hbm, rows_hbm, cols_hbm, count_hbm, kslot_hbm, agg_hbm, out_ref,
    small, count_v, agg_v, plan_v, plan_s, from_v, from_s, agp, a_v, side, summed,
    pan, colp, flip, colb, mids, terms, packed, snd, rcv,
    in_sem, a_sem, plan_sem, from_sem, p_send, p_recv, g_send, g_recv, c_send, c_recv, x_send, x_recv,
):
    bw = p_hbm.shape[0]
    dev_rows = agg_v.shape[1]
    rows_group = n_col * dev_rows
    slots = small.shape[2]
    ratio = n_col // n_row
    per = n_col // ratio
    cols_group = per * dev_rows
    hi = n_col // LO
    half = bw // 2
    row = lax.axis_index("row")
    me = lax.axis_index("col")
    z, x = me // LO, lax.rem(me, LO)
    partner = z * LO + (1 - x)
    root = me // ratio
    part = lax.rem(me, ratio)
    is_root = row == root
    alike = lax.rem(row, 2) == lax.rem(root, 2)
    is_head = alike & jnp.logical_not(is_root)
    twin_row = row + 1 - 2 * lax.rem(row, 2)

    def col_of(d):
        return lax.rem(me + d, n_col)

    def row_of(d):
        return lax.rem(row + d, n_row)

    def z_of(d):
        return jnp.bitwise_xor(z, d)

    barrier = pltpu.get_barrier_semaphore()
    for d in range(1, n_col):
        pl.semaphore_signal(barrier, inc=1, device_id=(row, col_of(d)), device_id_type=MESH)
    for d in range(1, n_row):
        pl.semaphore_signal(barrier, inc=1, device_id=(row_of(d), me), device_id_type=MESH)
    loads = [
        pltpu.make_async_copy(src, dst, in_sem.at[i])
        for i, (src, dst) in enumerate(
            [
                (agg_hbm, agg_v),
                (rows_hbm, small.at[0]),
                (cols_hbm, small.at[1]),
                (count_hbm, count_v),
                (kslot_hbm, small.at[2]),
                (p_hbm, pan.at[me]),
            ]
        )
    ]
    for c in loads:
        c.start()
    pl.semaphore_wait(barrier, n_col + n_row - 2)

    def remote(src, dst, s, r, dev):
        return pltpu.make_async_remote_copy(
            src_ref=src, dst_ref=dst, send_sem=s, recv_sem=r, device_id=dev, device_id_type=MESH
        )

    def send_own(do):
        def to(at, target, side):
            do(remote(p_hbm, pan.at[me], p_send.at[at], p_recv.at[me], (row, target * LO + side)))

        @pl.when(row != z)
        def _():
            to(0, row, me // per)

        for d in range(1, hi):
            @pl.when(z_of(d) != row)
            def _():
                to(d, z_of(d), x)

    own = [remote(p_hbm, pan.at[me], p_send.at[3 * hi - 1], p_recv.at[me], (row, partner))]
    own[0].start()
    send_own(lambda c: c.start())

    def panel_copies(q, src):
        m = lax.rem(q, per)
        copies = [remote(src, colp.at[m], c_send.at[m, 0], c_recv.at[m], (twin_row, me))]
        for d in range(1, n_row // 2):
            copies.append(
                remote(src, colp.at[m], c_send.at[m, d], c_recv.at[m], (row_of(2 * d), me))
            )
        return copies

    def twin_copy(m):
        return remote(colp.at[m], colp.at[m], c_send.at[m, 0], c_recv.at[m], (twin_row, me))

    def panel_landed(m):
        remote(
            p_hbm, colp.at[m], c_send.at[m, 0], c_recv.at[m], (row, partner)
        ).wait_recv()

    def hand_on(q, src):
        @pl.when(is_root & (q // per == part))
        def _():
            for c in reversed(panel_copies(q, src)):
                c.start()

    hand_on(me, p_hbm)

    @pl.loop(0, slots // 16)
    def _(g):
        for u in range(8):
            i = g * 8 + u
            lanes = pl.ds(pl.multiple_of(i * (2 * bw), 2 * bw), 2 * bw)
            pltpu.make_async_copy(a_hbm.at[:, lanes], a_v.at[i], a_sem).start()

    loads[0].wait()
    square = (dev_rows, dev_rows)
    eye = iota(square, 0) == iota(square, 1)
    mine = jnp.where(eye, jnp.broadcast_to(agg_v[...], square), 0)
    mine = jnp.sum(mine, axis=1, keepdims=True)
    agp[me] = jnp.broadcast_to(mine, agp.shape[1:])
    marks = [
        remote(agp.at[me], agp.at[me], g_send.at[d - 1], g_recv.at[me], (row, col_of(d)))
        for d in range(1, n_col)
    ]
    for c in marks:
        c.start()
    for c in loads[1:]:
        c.wait()
    make_plan(rows_group, cols_group, ratio, small, count_v, plan_v)
    plan_copy = pltpu.make_async_copy(plan_v, plan_s, plan_sem)
    plan_copy.start()
    lanes = iota((bw, 2 * bw), 1)
    side[0] = (lanes < bw).astype(F32).astype(BF16)
    side[1] = (lanes >= bw).astype(F32).astype(BF16)
    summed[slots] = jnp.zeros((bw, 2 * bw), BF16)

    def landed(q):
        remote(p_hbm, pan.at[q], p_send.at[0], p_recv.at[q], (row, partner)).wait_recv()

    blank = jnp.zeros((bw, bw), BF16)

    def turn(q):
        for h in range(dev_rows // 2):
            t = pan[q, :, 2 * h * bw:2 * (h + 1) * bw].T
            for e in range(2):
                block, at = t[e * bw:(e + 1) * bw], q * dev_rows + 2 * h + e
                flip[2 * at] = jnp.concatenate([block, blank], axis=1)
                flip[2 * at + 1] = jnp.concatenate([blank, block], axis=1)

    pltpu.make_async_copy(a_v, a_v, a_sem).wait()

    plan_copy.wait()

    def sums(lo, hi_, acc):
        def body(i, acc):
            for u in range(8):
                word = plan_s[i >> 4, ((i & 15) << 3) + u]
                keep = ((word >> 15) & 1).astype(F32)
                pair = a_v[(word & (slots - 1)) >> 1] * side[word & 1]
                acc = acc * keep + pair.astype(F32)
                summed[8 * i + u] = acc.astype(BF16)
            return acc

        return lax.fori_loop(lo, hi_, body, acc)

    turn(me)
    acc = sums(0, slots // 16, jnp.zeros((bw, 2 * bw), F32))
    landed(partner)
    hand_on(partner, pan.at[partner])
    def pair(d):
        q = z_of(d) * LO + x
        return q, q + 1 - 2 * x, is_root & (q // per == x)

    def relay(q, at):
        return remote(pan.at[q], pan.at[q], p_send.at[at], p_recv.at[q], (row, partner))

    for d in range(1, hi):
        q, other, both = pair(d)

        @pl.when(both | jnp.logical_not(is_root))
        def _():
            landed(q)
            relay(q, hi - 1 + d).start()
            hand_on(q, pan.at[q])

        @pl.when(both)
        def _():
            landed(other)
            relay(other, 2 * hi - 1 + d).start()
            hand_on(other, pan.at[other])

    def unpack(m, src):
        for b in range(dev_rows):
            colb[m * dev_rows + b] = src[:, b * bw:(b + 1) * bw]

    @pl.when(is_root)
    def _():
        for m in range(per):
            unpack(m, pan.at[part * per + m])

    turn(partner)
    for d in range(1, hi):
        q, other, both = pair(d)

        @pl.when(both | jnp.logical_not(is_root))
        def _():
            turn(q)

        @pl.when(both)
        def _():
            turn(other)

    acc = sums(slots // 16, slots // 8, acc)
    cells, lists = slots // 128, slots // 128 + KC * AGG * AGG // 128

    def listed(p, m):
        return plan_s[lists, p * AGG + m]

    part_groups = KC // ratio

    def mid(h):
        for g in range(part_groups):
            p = h * part_groups + g
            left = jnp.concatenate(
                [
                    flip[2 * (listed(p, 2 * h) & (rows_group - 1))]
                    + flip[2 * (listed(p, 2 * h + 1) & (rows_group - 1)) + 1]
                    for h in range(AGG // 2)
                ],
                axis=1,
            )

            def cell(m, n):
                at = (p * AGG + m) * AGG + n
                return summed[plan_s[cells + (at >> 7), at & 127]]

            mat = jnp.concatenate(
                [jnp.concatenate([cell(m, n) for n in range(AGG)], axis=1) for m in range(AGG)], axis=0
            )
            mids[p] = jnp.dot(left, mat, preferred_element_type=F32).astype(BF16)

    near = z // (hi // ratio)

    for d in range(1, hi // ratio):
        q, other, both = pair(d)

        @pl.when(is_root & jnp.logical_not(both))
        def _():
            landed(q)
            turn(q)

        @pl.when(jnp.logical_not(both))
        def _():
            landed(other)
            turn(other)

    is_mate = twin_row == root

    @pl.when(is_mate)
    def _():
        for m in range(per):
            panel_landed(m)
            unpack(m, colp.at[m])

    mid(near)
    for d in range(hi // ratio, hi):
        q, other, both = pair(d)

        @pl.when(is_root & jnp.logical_not(both))
        def _():
            landed(q)
            turn(q)

        @pl.when(jnp.logical_not(both))
        def _():
            landed(other)
            turn(other)

    @pl.when(is_head)
    def _():
        for m in range(per):
            panel_landed(m)
            twin_copy(m).start()

    for h in range(1, ratio):
        mid(lax.rem(near + h, ratio))
    for d in range(1, n_col):
        q = col_of(d)
        remote(agp.at[q], agp.at[q], g_send.at[0], g_recv.at[q], (row, partner)).wait_recv()

    row_marks = jnp.concatenate([agp[c] for c in range(n_col)], axis=0)
    there = iota((rows_group, 2 * bw), 0) == small[0, 0:1, 0:1]
    first = jnp.sum(jnp.where(there, row_marks, 0), axis=0, keepdims=True)
    first = first * KC + small[2, 0:1, 0:1]
    owner = iota((1, 2 * bw), 1)
    slot = (first - KC * owner + 8 * n_col * n_col) & (n_col - 1)
    holds = (owner >> bits(per)) * (KC // ratio) + (slot >> bits(ratio))
    from_v[...] = jnp.where(slot < KC, holds, 0)
    from_copy = pltpu.make_async_copy(from_v, from_s, from_sem)
    from_copy.start()
    for m in range(per):
        @pl.when(jnp.logical_not(is_root | is_mate))
        def _():
            @pl.when(jnp.logical_not(is_head))
            def _():
                panel_landed(m)

            unpack(m, colp.at[m])

    for p in range(KC):
        right = jnp.concatenate(
            [colb[(listed(p, n // 2) >> 16) & (cols_group - 1)] for n in range(2 * AGG)], axis=0
        )
        terms[p] = jnp.dot(mids[p], right, preferred_element_type=F32)
    for p in range(KC):
        even = terms[p, pl.ds(0, half, stride=2), :]
        odd = terms[p, pl.ds(1, half, stride=2), :]
        packed[p] = jnp.concatenate([even, odd], axis=1).astype(BF16)
    from_copy.wait()
    for o in range(n_col):
        snd[o] = packed[within(from_s[0, o], KC)]

    def term(o):
        return remote(snd.at[o], rcv.at[me], x_send.at[o], x_recv.at[me], (row, o))

    for o in range(n_col):
        @pl.when(me != o)
        def _():
            term(o).start()

    rcv[me] = snd[me]
    for d in range(1, n_col):
        q = col_of(d)
        remote(snd.at[0], rcv.at[q], x_send.at[0], x_recv.at[q], (row, partner)).wait_recv()
    total = [jnp.zeros((half, 2 * bw), F32) for _ in range(KC)]
    for c in range(n_col):
        value = rcv[c].astype(F32)
        where = (first + (c - (KC + 1) * me + 8 * n_col * n_col)) & (n_col - 1)
        for k in range(KC):
            total[k] += jnp.where(where == k, value, 0.0)
    for k in range(KC):
        out_ref[k * half:(k + 1) * half, :] = total[k].astype(BF16)

    for c in own + marks:
        c.wait_send()
    for d in range(1, hi):
        q, other, both = pair(d)

        @pl.when(both | jnp.logical_not(is_root))
        def _():
            relay(q, hi - 1 + d).wait_send()

        @pl.when(both)
        def _():
            relay(other, 2 * hi - 1 + d).wait_send()

    send_own(lambda c: c.wait_send())
    for o in range(n_col):
        @pl.when(me != o)
        def _():
            term(o).wait_send()

    @pl.when(is_root)
    def _():
        for m in range(per):
            for c in panel_copies(m, pan.at[0]):
                c.wait_send()

    @pl.when(is_head)
    def _():
        for m in range(per):
            twin_copy(m).wait_send()


def hbm(value):
    return pltpu.with_memory_space_constraint(value, pltpu.HBM)


def on_device(n_row, n_col, a_vals, p_vals, a_rows, a_cols, a_count, c_slot, agg):
    bw = p_vals.shape[0]
    dev_rows = agg.shape[0]
    slots = a_rows.shape[1]
    rows_group = dev_rows * n_col
    ratio = n_col // n_row
    per = n_col // ratio
    cols_group = per * dev_rows
    hi = n_col // LO
    assert rows_group // AGG == n_col and n_col >= KC and n_row % 2 == 0
    assert ratio == LO and hi == n_row
    assert math.gcd(KC, n_col) == ratio and slots % 128 == 0 and 2 * bw == 128
    assert all(n & (n - 1) == 0 for n in (n_col, slots, cols_group, dev_rows, hi))
    keep = pl.BlockSpec(memory_space=pltpu.HBM)
    vmem = pl.BlockSpec(memory_space=pltpu.VMEM)
    dma = pltpu.SemaphoreType.DMA
    out = pl.pallas_call(
        functools.partial(kernel, n_row, n_col),
        out_shape=jax.ShapeDtypeStruct((KC * bw // 2, 2 * bw), BF16),
        in_specs=[keep] * 7,
        out_specs=vmem,
        scratch_shapes=[
            pltpu.VMEM((3, 1, slots), I32),
            pltpu.VMEM((1, 1), I32),
            pltpu.VMEM((1, dev_rows), I32),
            pltpu.VMEM((8, 128), I32),
            pltpu.SMEM((8, 128), I32),
            pltpu.VMEM((1, 128), I32),
            pltpu.SMEM((1, 128), I32),
            pltpu.VMEM((n_col, dev_rows, 128), I32),
            pltpu.VMEM((slots // 2, bw, 2 * bw), BF16),
            pltpu.VMEM((2, bw, 2 * bw), BF16),
            pltpu.VMEM((slots + 1, bw, 2 * bw), BF16),
            pltpu.VMEM((n_col, bw, dev_rows * bw), BF16),
            pltpu.VMEM((per, bw, dev_rows * bw), BF16),
            pltpu.VMEM((2 * rows_group, bw, 2 * bw), BF16),
            pltpu.VMEM((cols_group, bw, bw), BF16),
            pltpu.VMEM((KC, bw, 2 * AGG * bw), BF16),
            pltpu.VMEM((KC, bw, bw), F32),
            pltpu.VMEM((KC, bw // 2, 2 * bw), BF16),
            pltpu.VMEM((n_col, bw // 2, 2 * bw), BF16),
            pltpu.VMEM((n_col, bw // 2, 2 * bw), BF16),
            dma((6,)), dma, dma, dma,
            dma((3 * hi,)), dma((n_col,)),
            dma((n_col,)), dma((n_col,)),
            dma((per, n_row // 2)), dma((per,)),
            dma((n_col,)), dma((n_col,)),
        ],
        compiler_params=pltpu.CompilerParams(
            collective_id=0, has_side_effects=True, vmem_limit_bytes=40 * 1024 * 1024
        ),
    )(
        hbm(a_vals), hbm(p_vals), hbm(a_rows), hbm(a_cols), a_count, hbm(c_slot),
        hbm(agg.reshape(1, dev_rows)),
    )
    return out.astype(F32).reshape(1, KC * bw * bw)


def solution(mesh):
    return jax.shard_map(
        functools.partial(on_device, mesh.shape["row"], mesh.shape["col"]),
        mesh=mesh,
        in_specs=(
            P("row", "col"),
            P(None, ("row", "col")),
            P("row", "col"),
            P("row", "col"),
            P("row", "col"),
            P("row", "col"),
            P(("row", "col")),
        ),
        out_specs=P(("row", "col"), None),
        check_vma=False,
    )
```

```python
import functools
import math

import jax
import jax.numpy as jnp
from jax import lax
from jax.experimental import pallas as pl
from jax.experimental.pallas import tpu as pltpu
from jax.sharding import PartitionSpec as P

AGG = 8
KC = 6
LO = 2
MESH = pl.DeviceIdType.MESH
F32 = jnp.float32
BF16 = jnp.bfloat16
I32 = jnp.int32


def iota(shape, dim):
    return lax.broadcasted_iota(I32, shape, dim)


def within(at, size):
    return jnp.minimum(jnp.maximum(at, 0), size - 1)


def bits(n):
    return n.bit_length() - 1


def make_plan(rows_group, cols_group, ratio, small, count_v, plan_v):
    slots = small.shape[2]
    rb, cb, sb, ab = bits(rows_group), bits(cols_group), bits(slots), bits(AGG)
    groups = KC
    rows, cols = small[0], small[1]
    lane = iota((1, slots), 1)
    group = (rows >> cb) * (KC // ratio) + (small[2] >> bits(ratio))
    group = jnp.where(lane < count_v[...], group, groups)
    key = ((((group << rb) | rows) << cb | cols) << sb) | lane
    across = jnp.broadcast_to(key, (slots, slots))
    side, place = iota((slots, slots), 0), iota((slots, slots), 1)
    down = jnp.sum(jnp.where(side == place, across, 0), axis=1, keepdims=True)
    less = across < down
    rank = jnp.sum(jnp.where(less, 1, 0), axis=1, keepdims=True)
    cell_a, cell_d = key >> sb, down >> sb
    more = jnp.sum(jnp.where((cell_a == cell_d) & (across > down), 1, 0), axis=1, keepdims=True)
    word = jnp.sum(jnp.where(rank == place, down, 0), axis=0, keepdims=True)
    top = word >> sb
    same = (top == pltpu.roll(top, 1, 1)) & (lane > 0)
    word = (word & (slots - 1)) | (same.astype(I32) << 15)
    for g in range(slots // 128):
        plan_v[g:g + 1, :] = word[:, g * 128:(g + 1) * 128]

    def spots(line, n):
        line_a = (group << n) | line
        line_d = jnp.sum(jnp.where(side == place, line_a, 0), axis=1, keepdims=True)
        other = jnp.where((line_d == line_a) & (down < across), 1, 0)
        line_a = jnp.where(jnp.sum(other, axis=0, keepdims=True) == 0, line_a, -1)
        mine = (line_a < line_d) & (line_a >= (line_d >> n) << n)
        return line_d, jnp.sum(jnp.where(mine, 1, 0), axis=1, keepdims=True)

    line, down_at = spots(rows, rb)
    post, over_at = spots(cols, cb)
    group = line >> rb
    cell = (((group << ab) | down_at) << ab) | over_at
    tag = jnp.where((more == 0) & (group < groups), rank + 1, 0)
    at = slots // 128
    q = iota((slots, 128), 1)
    for g in range(groups * AGG * AGG // 128):
        found = jnp.sum(jnp.where(cell == q + g * 128, tag, 0), axis=0, keepdims=True)
        plan_v[at + g:at + g + 1, :] = jnp.where(found > 0, found - 1, slots)
    at += groups * AGG * AGG // 128
    line = jnp.where((group << ab) + down_at == q, line & (rows_group - 1), 0)
    post = jnp.where((group << ab) + over_at == q, post & (cols_group - 1), 0)
    line = jnp.max(line, axis=0, keepdims=True)
    post = jnp.max(post, axis=0, keepdims=True)
    plan_v[at:at + 1, :] = line | (post << 16)


def kernel(
    n_row, n_col, a_hbm, p_hbm, rows_hbm, cols_hbm, count_hbm, kslot_hbm, agg_hbm, out_ref,
    small, count_v, agg_v, plan_v, plan_s, from_v, from_s, agp, a_v, side, summed,
    pan, colp, flip, colb, mids, terms, packed, snd, rcv,
    in_sem, a_sem, plan_sem, from_sem, p_send, p_recv, g_send, g_recv, c_send, c_recv, x_send, x_recv,
):
    bw = p_hbm.shape[0]
    dev_rows = agg_v.shape[1]
    rows_group = n_col * dev_rows
    slots = small.shape[2]
    ratio = n_col // n_row
    per = n_col // ratio
    cols_group = per * dev_rows
    hi = n_col // LO
    half = bw // 2
    row = lax.axis_index("row")
    me = lax.axis_index("col")
    z, x = me // LO, lax.rem(me, LO)
    partner = z * LO + (1 - x)
    root = me // ratio
    part = lax.rem(me, ratio)
    is_root = row == root
    alike = lax.rem(row, 2) == lax.rem(root, 2)
    is_head = alike & jnp.logical_not(is_root)
    twin_row = row + 1 - 2 * lax.rem(row, 2)

    def col_of(d):
        return lax.rem(me + d, n_col)

    def row_of(d):
        return lax.rem(row + d, n_row)

    def z_of(d):
        return jnp.bitwise_xor(z, d)

    barrier = pltpu.get_barrier_semaphore()
    for d in range(1, n_col):
        pl.semaphore_signal(barrier, inc=1, device_id=(row, col_of(d)), device_id_type=MESH)
    for d in range(1, n_row):
        pl.semaphore_signal(barrier, inc=1, device_id=(row_of(d), me), device_id_type=MESH)
    loads = [
        pltpu.make_async_copy(src, dst, in_sem.at[i])
        for i, (src, dst) in enumerate(
            [
                (agg_hbm, agg_v),
                (rows_hbm, small.at[0]),
                (cols_hbm, small.at[1]),
                (count_hbm, count_v),
                (kslot_hbm, small.at[2]),
                (p_hbm, pan.at[me]),
            ]
        )
    ]
    for c in loads:
        c.start()
    pl.semaphore_wait(barrier, n_col + n_row - 2)

    def remote(src, dst, s, r, dev):
        return pltpu.make_async_remote_copy(
            src_ref=src, dst_ref=dst, send_sem=s, recv_sem=r, device_id=dev, device_id_type=MESH
        )

    def send_own(do):
        def to(at, target, side):
            do(remote(p_hbm, pan.at[me], p_send.at[at], p_recv.at[me], (row, target * LO + side)))

        @pl.when(row != z)
        def _():
            to(0, row, me // per)

        for d in range(1, hi):
            @pl.when(z_of(d) != row)
            def _():
                to(d, z_of(d), x)

    own = [remote(p_hbm, pan.at[me], p_send.at[3 * hi - 1], p_recv.at[me], (row, partner))]
    own[0].start()
    send_own(lambda c: c.start())

    def panel_copies(q, src):
        m = lax.rem(q, per)
        copies = [remote(src, colp.at[m], c_send.at[m, 0], c_recv.at[m], (twin_row, me))]
        for d in range(1, n_row // 2):
            copies.append(
                remote(src, colp.at[m], c_send.at[m, d], c_recv.at[m], (row_of(2 * d), me))
            )
        return copies

    def twin_copy(m):
        return remote(colp.at[m], colp.at[m], c_send.at[m, 0], c_recv.at[m], (twin_row, me))

    def panel_landed(m):
        remote(
            p_hbm, colp.at[m], c_send.at[m, 0], c_recv.at[m], (row, partner)
        ).wait_recv()

    def hand_on(q, src):
        @pl.when(is_root & (q // per == part))
        def _():
            for c in reversed(panel_copies(q, src)):
                c.start()

    hand_on(me, p_hbm)

    @pl.loop(0, slots // 16)
    def _(g):
        for u in range(8):
            i = g * 8 + u
            lanes = pl.ds(pl.multiple_of(i * (2 * bw), 2 * bw), 2 * bw)
            pltpu.make_async_copy(a_hbm.at[:, lanes], a_v.at[i], a_sem).start()

    loads[0].wait()
    square = (dev_rows, dev_rows)
    eye = iota(square, 0) == iota(square, 1)
    mine = jnp.where(eye, jnp.broadcast_to(agg_v[...], square), 0)
    mine = jnp.sum(mine, axis=1, keepdims=True)
    agp[me] = jnp.broadcast_to(mine, agp.shape[1:])
    marks = [
        remote(agp.at[me], agp.at[me], g_send.at[d - 1], g_recv.at[me], (row, col_of(d)))
        for d in range(1, n_col)
    ]
    for c in marks:
        c.start()
    for c in loads[1:]:
        c.wait()
    make_plan(rows_group, cols_group, ratio, small, count_v, plan_v)
    plan_copy = pltpu.make_async_copy(plan_v, plan_s, plan_sem)
    plan_copy.start()
    lanes = iota((bw, 2 * bw), 1)
    side[0] = (lanes < bw).astype(F32).astype(BF16)
    side[1] = (lanes >= bw).astype(F32).astype(BF16)
    summed[slots] = jnp.zeros((bw, 2 * bw), BF16)

    def landed(q):
        remote(p_hbm, pan.at[q], p_send.at[0], p_recv.at[q], (row, partner)).wait_recv()

    blank = jnp.zeros((bw, bw), BF16)

    def turn(q):
        for h in range(dev_rows // 2):
            t = pan[q, :, 2 * h * bw:2 * (h + 1) * bw].T
            for e in range(2):
                block, at = t[e * bw:(e + 1) * bw], q * dev_rows + 2 * h + e
                flip[2 * at] = jnp.concatenate([block, blank], axis=1)
                flip[2 * at + 1] = jnp.concatenate([blank, block], axis=1)

    pltpu.make_async_copy(a_v, a_v, a_sem).wait()

    plan_copy.wait()

    def sums(lo, hi_, acc):
        def body(i, acc):
            for u in range(8):
                word = plan_s[i >> 4, ((i & 15) << 3) + u]
                keep = ((word >> 15) & 1).astype(F32)
                pair = a_v[(word & (slots - 1)) >> 1] * side[word & 1]
                acc = acc * keep + pair.astype(F32)
                summed[8 * i + u] = acc.astype(BF16)
            return acc

        return lax.fori_loop(lo, hi_, body, acc)

    turn(me)
    acc = sums(0, slots // 16, jnp.zeros((bw, 2 * bw), F32))
    landed(partner)
    hand_on(partner, pan.at[partner])
    def pair(d):
        q = z_of(d) * LO + x
        return q, q + 1 - 2 * x, is_root & (q // per == x)

    def relay(q, at):
        return remote(pan.at[q], pan.at[q], p_send.at[at], p_recv.at[q], (row, partner))

    for d in range(1, hi):
        q, other, both = pair(d)

        @pl.when(both | jnp.logical_not(is_root))
        def _():
            landed(q)
            relay(q, hi - 1 + d).start()
            hand_on(q, pan.at[q])

        @pl.when(both)
        def _():
            landed(other)
            relay(other, 2 * hi - 1 + d).start()
            hand_on(other, pan.at[other])

        if d == 1:
            turn(partner)
            acc = sums(slots // 16, slots // 8, acc)

    def unpack(m, src):
        for b in range(dev_rows):
            colb[m * dev_rows + b] = src[:, b * bw:(b + 1) * bw]

    @pl.when(is_root)
    def _():
        for m in range(per):
            unpack(m, pan.at[part * per + m])

    for d in range(1, hi):
        q, other, both = pair(d)

        @pl.when(both | jnp.logical_not(is_root))
        def _():
            turn(q)

        @pl.when(both)
        def _():
            turn(other)

    cells, lists = slots // 128, slots // 128 + KC * AGG * AGG // 128

    def listed(p, m):
        return plan_s[lists, p * AGG + m]

    part_groups = KC // ratio

    def mid(h):
        for g in range(part_groups):
            p = h * part_groups + g
            fold = 128 // (AGG * AGG)
            line, lane = cells + p // fold, p % fold * (AGG * AGG)
            left = jnp.concatenate(
                [
                    flip[2 * (listed(p, 2 * h) & (rows_group - 1))]
                    + flip[2 * (listed(p, 2 * h + 1) & (rows_group - 1)) + 1]
                    for h in range(AGG // 2)
                ],
                axis=1,
            )

            def cell(m, n):
                return summed[plan_s[line, lane + m * AGG + n]]

            mat = jnp.concatenate(
                [jnp.concatenate([cell(m, n) for n in range(AGG)], axis=1) for m in range(AGG)], axis=0
            )
            mids[p] = jnp.dot(left, mat, preferred_element_type=F32).astype(BF16)

    near = z // (hi // ratio)

    for d in range(1, hi // ratio):
        q, other, both = pair(d)

        @pl.when(is_root & jnp.logical_not(both))
        def _():
            landed(q)
            turn(q)

        @pl.when(jnp.logical_not(both))
        def _():
            landed(other)
            turn(other)

    is_mate = twin_row == root

    @pl.when(is_mate)
    def _():
        for m in range(per):
            panel_landed(m)
            unpack(m, colp.at[m])

    for h in range(ratio):
        pl.when(near == h)(functools.partial(mid, h))
    for d in range(1, n_col):
        q = col_of(d)
        remote(agp.at[q], agp.at[q], g_send.at[0], g_recv.at[q], (row, partner)).wait_recv()

    row_marks = jnp.concatenate([agp[c] for c in range(n_col)], axis=0)
    there = iota((rows_group, 2 * bw), 0) == small[0, 0:1, 0:1]
    first = jnp.sum(jnp.where(there, row_marks, 0), axis=0, keepdims=True)
    first = first * KC + small[2, 0:1, 0:1]
    owner = iota((1, 2 * bw), 1)
    slot = (first - KC * owner + 8 * n_col * n_col) & (n_col - 1)
    holds = (owner >> bits(per)) * (KC // ratio) + (slot >> bits(ratio))
    from_v[...] = jnp.where(slot < KC, holds, 0)
    from_copy = pltpu.make_async_copy(from_v, from_s, from_sem)
    from_copy.start()
    for d in range(hi // ratio, hi):
        q, other, both = pair(d)

        @pl.when(is_root & jnp.logical_not(both))
        def _():
            landed(q)
            turn(q)

        @pl.when(jnp.logical_not(both))
        def _():
            landed(other)
            turn(other)

    @pl.when(is_head)
    def _():
        for m in range(per):
            panel_landed(m)
            twin_copy(m).start()

    for h in range(ratio):
        pl.when(near != h)(functools.partial(mid, h))
    for m in range(per):
        @pl.when(jnp.logical_not(is_root | is_mate))
        def _():
            @pl.when(jnp.logical_not(is_head))
            def _():
                panel_landed(m)

            unpack(m, colp.at[m])

    for p in range(KC):
        right = jnp.concatenate(
            [colb[(listed(p, n // 2) >> 16) & (cols_group - 1)] for n in range(2 * AGG)], axis=0
        )
        terms[p] = jnp.dot(mids[p], right, preferred_element_type=F32)
    for p in range(KC):
        even = terms[p, pl.ds(0, half, stride=2), :]
        odd = terms[p, pl.ds(1, half, stride=2), :]
        packed[p] = jnp.concatenate([even, odd], axis=1).astype(BF16)
    from_copy.wait()
    for o in range(n_col):
        snd[o] = packed[within(from_s[0, o], KC)]

    def term(o):
        return remote(snd.at[o], rcv.at[me], x_send.at[o], x_recv.at[me], (row, o))

    for o in range(n_col):
        @pl.when(me != o)
        def _():
            term(o).start()

    rcv[me] = snd[me]
    for d in range(1, n_col):
        q = col_of(d)
        remote(snd.at[0], rcv.at[q], x_send.at[0], x_recv.at[q], (row, partner)).wait_recv()
    total = [jnp.zeros((half, 2 * bw), F32) for _ in range(KC)]
    for c in range(n_col):
        value = rcv[c].astype(F32)
        where = (first + (c - (KC + 1) * me + 8 * n_col * n_col)) & (n_col - 1)
        for k in range(KC):
            total[k] += jnp.where(where == k, value, 0.0)
    for k in range(KC):
        out_ref[k * half:(k + 1) * half, :] = total[k].astype(BF16)

    for c in own + marks:
        c.wait_send()
    for d in range(1, hi):
        q, other, both = pair(d)

        @pl.when(both | jnp.logical_not(is_root))
        def _():
            relay(q, hi - 1 + d).wait_send()

        @pl.when(both)
        def _():
            relay(other, 2 * hi - 1 + d).wait_send()

    send_own(lambda c: c.wait_send())
    for o in range(n_col):
        @pl.when(me != o)
        def _():
            term(o).wait_send()

    @pl.when(is_root)
    def _():
        for m in range(per):
            for c in panel_copies(m, pan.at[0]):
                c.wait_send()

    @pl.when(is_head)
    def _():
        for m in range(per):
            twin_copy(m).wait_send()


def hbm(value):
    return pltpu.with_memory_space_constraint(value, pltpu.HBM)


def on_device(n_row, n_col, a_vals, p_vals, a_rows, a_cols, a_count, c_slot, agg):
    bw = p_vals.shape[0]
    dev_rows = agg.shape[0]
    slots = a_rows.shape[1]
    rows_group = dev_rows * n_col
    ratio = n_col // n_row
    per = n_col // ratio
    cols_group = per * dev_rows
    hi = n_col // LO
    assert rows_group // AGG == n_col and n_col >= KC and n_row % 2 == 0
    assert ratio == LO and hi == n_row
    assert math.gcd(KC, n_col) == ratio and slots % 128 == 0 and 2 * bw == 128
    assert all(n & (n - 1) == 0 for n in (n_col, slots, cols_group, dev_rows, hi))
    keep = pl.BlockSpec(memory_space=pltpu.HBM)
    vmem = pl.BlockSpec(memory_space=pltpu.VMEM)
    dma = pltpu.SemaphoreType.DMA
    out = pl.pallas_call(
        functools.partial(kernel, n_row, n_col),
        out_shape=jax.ShapeDtypeStruct((KC * bw // 2, 2 * bw), BF16),
        in_specs=[keep] * 7,
        out_specs=vmem,
        scratch_shapes=[
            pltpu.VMEM((3, 1, slots), I32),
            pltpu.VMEM((1, 1), I32),
            pltpu.VMEM((1, dev_rows), I32),
            pltpu.VMEM((8, 128), I32),
            pltpu.SMEM((8, 128), I32),
            pltpu.VMEM((1, 128), I32),
            pltpu.SMEM((1, 128), I32),
            pltpu.VMEM((n_col, dev_rows, 128), I32),
            pltpu.VMEM((slots // 2, bw, 2 * bw), BF16),
            pltpu.VMEM((2, bw, 2 * bw), BF16),
            pltpu.VMEM((slots + 1, bw, 2 * bw), BF16),
            pltpu.VMEM((n_col, bw, dev_rows * bw), BF16),
            pltpu.VMEM((per, bw, dev_rows * bw), BF16),
            pltpu.VMEM((2 * rows_group, bw, 2 * bw), BF16),
            pltpu.VMEM((cols_group, bw, bw), BF16),
            pltpu.VMEM((KC, bw, 2 * AGG * bw), BF16),
            pltpu.VMEM((KC, bw, bw), F32),
            pltpu.VMEM((KC, bw // 2, 2 * bw), BF16),
            pltpu.VMEM((n_col, bw // 2, 2 * bw), BF16),
            pltpu.VMEM((n_col, bw // 2, 2 * bw), BF16),
            dma((6,)), dma, dma, dma,
            dma((3 * hi,)), dma((n_col,)),
            dma((n_col,)), dma((n_col,)),
            dma((per, n_row // 2)), dma((per,)),
            dma((n_col,)), dma((n_col,)),
        ],
        compiler_params=pltpu.CompilerParams(
            collective_id=0, has_side_effects=True, vmem_limit_bytes=40 * 1024 * 1024
        ),
    )(
        hbm(a_vals), hbm(p_vals), hbm(a_rows), hbm(a_cols), a_count, hbm(c_slot),
        hbm(agg.reshape(1, dev_rows)),
    )
    return out.astype(F32).reshape(1, KC * bw * bw)


def solution(mesh):
    return jax.shard_map(
        functools.partial(on_device, mesh.shape["row"], mesh.shape["col"]),
        mesh=mesh,
        in_specs=(
            P("row", "col"),
            P(None, ("row", "col")),
            P("row", "col"),
            P("row", "col"),
            P("row", "col"),
            P("row", "col"),
            P(("row", "col")),
        ),
        out_specs=P(("row", "col"), None),
        check_vma=False,
    )
```
